32 devices in a mesh: slab: 8 (over z, x), energy: 4 (over y, core).
Axes of the slice: x: 2, y: 2, z: 4, core: 2. Of those that a mesh axis runs over, the one named last changes fastest.
Arguments:
- energy_sq: float32 [4], P('energy'), may hold values from 2.5 to 3.3
- broadening: float32 [4], P('energy'), may hold values from 0.05 to 0.1
- onsite: float32 [8, 192, 192], P('slab'), may hold values from -0.005051815 to 2
- coupling: float32 [8, 192, 192], P('slab'), may hold values from -0.005051815 to 0.005051815
- sigma_in: float32 [4, 8, 192, 384], P('energy', 'slab'), may hold values from -0.02 to 0.005051815
- anharmonic: float32 [8, 192, 192], P('slab'), may hold values from 0.5 to 2
- energy_pairs: int32 [4, 8, 2], P('energy'), may hold values from 0 to 3
Outputs:
- green_diag: float32 [4, 8, 192, 384], P('energy', 'slab')
- sigma_out: float32 [4, 8, 192, 384], P('energy', 'slab')
The draws below stay inside these ranges and needn't reach their ends.
All inputs are finite; a program needn't handle non-finite values.
Results may differ from the reference program's by a relative error of at most 0.0003.
Values sent between devices are 32-bit elements; how exact they have to be, the bound alone decides.
No kernel may reach another device: no remote copies, remote signals or barrier semaphores. Data moves between devices by JAX's collectives and lax.ppermute only.
A program may use at most 128 MiB of HBM per device.

```python
import math
import jax
import jax.numpy as jnp
from jax import lax

W = 192
PAIRS = 8
SLABS = 8
ENERGIES = 4


def symmetric(values):
    return 0.5 * (values + jnp.swapaxes(values, -1, -2))


def draw_onsite(key, part):
    key_off = jax.random.fold_in(key, 11)
    key_diag = jax.random.fold_in(key, 12)
    bound_off = 0.07 / math.sqrt(W)
    off_part = symmetric(jax.random.uniform(key_off, (SLABS, W, W), jnp.float32, -bound_off, bound_off))
    diag_part = jax.random.uniform(key_diag, (SLABS, W), jnp.float32, 1.7, 2.0)
    identity = jnp.eye(W, dtype=jnp.float32)
    return off_part * (1.0 - identity) + diag_part[:, :, None] * identity


def draw_sigma_in(key, part):
    key_real = jax.random.fold_in(key, 21)
    key_imag = jax.random.fold_in(key, 22)
    key_diag = jax.random.fold_in(key, 23)
    bound_real = 0.07 / math.sqrt(W)
    real_part = symmetric(jax.random.uniform(key_real, (ENERGIES, SLABS, W, W), jnp.float32, -bound_real, bound_real))
    bound_imag = 0.02 / W
    identity = jnp.eye(W, dtype=jnp.float32)
    imag_off = symmetric(jax.random.uniform(key_imag, (ENERGIES, SLABS, W, W), jnp.float32, -bound_imag, bound_imag)) * (1.0 - identity)
    imag_diag = jax.random.uniform(key_diag, (ENERGIES, SLABS, W), jnp.float32, -0.02, 0.0)
    imag_part = imag_off + imag_diag[..., :, None] * identity
    return jnp.concatenate([real_part, imag_part], -1)


def set_ends(values, rng, smallest, high):
    longest = values.shape.index(max(values.shape))
    spots = []
    for shift in (0, 1):
        where = [jax.random.randint(jax.random.fold_in(rng, axis), (), 0, length) for axis, length in enumerate(values.shape)]
        where[longest] = (where[longest] + shift) % values.shape[longest]
        spots.append(tuple(where))
    return values.at[spots[0]].set(smallest).at[spots[1]].set(high)


def levels(rng, dims, pieces, least, top_value):
    def one(dim, shards_of):
        steps = jax.random.uniform(jax.random.fold_in(jax.random.fold_in(rng, 6), dim), (shards_of,), jnp.float32, least / len(pieces), top_value / len(pieces))
        return jnp.repeat(jnp.exp(steps), dims[dim] // shards_of).reshape((-1,) + (1,) * (len(dims) - dim - 1))

    level = one(*pieces[0])
    for cut in pieces[1:]:
        level = level * one(*cut)
    return level


def setup_inputs(seed: int = 0) -> dict:
    key_list = jax.random.split(jax.random.key(seed), 8)
    energy_sq = jnp.clip(2.5 + 0.79999995 * jax.random.uniform(key_list[0], (ENERGIES,), jnp.float32) ** levels(key_list[0], (ENERGIES,), ((0, 4),), -0.2, 0.2), 2.5, 3.3)
    broadening = jnp.clip(jnp.exp(math.log(0.1) - 0.6931472 * jax.random.uniform(key_list[1], (ENERGIES,), jnp.float32) ** levels(key_list[1], (ENERGIES,), ((0, 4),), -0.2, 0.2)), 0.05, 0.1)
    onsite = draw_onsite(jax.random.fold_in(key_list[7], 71), 0)
    coupling = jnp.clip(jax.random.uniform(key_list[3], (SLABS, W, W), jnp.float32, -0.005051815, 0.005051815) * levels(key_list[3], (SLABS, W, W), ((0, 8),), -0.4, 0.0), -0.005051815, 0.005051815)
    sigma_in = draw_sigma_in(jax.random.fold_in(key_list[7], 71), 0)
    anharmonic = jnp.clip(jnp.exp(math.log(2.0) - 1.3862944 * jax.random.uniform(key_list[5], (SLABS, W, W), jnp.float32) ** levels(key_list[5], (SLABS, W, W), ((0, 8),), -0.2, 0.2)), 0.5, 2.0)
    energy_pairs = set_ends(jax.random.randint(key_list[6], (ENERGIES, PAIRS, 2), 0, ENERGIES), jax.random.fold_in(key_list[6], 1), 0, ENERGIES - 1).astype(jnp.int32)
    return {"energy_sq": energy_sq, "broadening": broadening, "onsite": onsite, "coupling": coupling, "sigma_in": sigma_in, "anharmonic": anharmonic, "energy_pairs": energy_pairs}


def complex_product(left, right):
    block_width = left.shape[-2]
    left_real = left[..., :block_width]
    left_imag = left[..., block_width:]
    right_real = right[..., :block_width]
    right_imag = right[..., block_width:]
    high = lax.Precision.HIGHEST
    real_part = jnp.einsum('...ij,...jk->...ik', left_real, right_real, precision=high) - jnp.einsum('...ij,...jk->...ik', left_imag, right_imag, precision=high)
    imag_part = jnp.einsum('...ij,...jk->...ik', left_real, right_imag, precision=high) + jnp.einsum('...ij,...jk->...ik', left_imag, right_real, precision=high)
    return jnp.concatenate([real_part, imag_part], -1)

def invert(matrix):
    block_width = matrix.shape[-2]
    high = lax.Precision.HIGHEST
    real_part = matrix[..., :block_width]
    imag_part = matrix[..., block_width:]
    real_part = 0.5 * (real_part + jnp.swapaxes(real_part, -1, -2))
    imag_part = 0.5 * (imag_part + jnp.swapaxes(imag_part, -1, -2))
    identity = jnp.broadcast_to(jnp.eye(block_width, dtype=jnp.float32), real_part.shape)
    imag_factor = jnp.linalg.cholesky(imag_part)
    factor_inverse = jax.scipy.linalg.solve_triangular(imag_factor, identity, lower=True)
    factor_trans = jnp.swapaxes(factor_inverse, -1, -2)
    middle = jnp.einsum('...ij,...jk,...kl->...il', factor_inverse, real_part, factor_trans, precision=high)
    middle = 0.5 * (middle + jnp.swapaxes(middle, -1, -2))
    squared = jnp.einsum('...ij,...jk->...ik', middle, middle, precision=high) + identity
    square_factor = jnp.linalg.cholesky(squared)
    right_side = jax.scipy.linalg.cho_solve((square_factor, True), factor_inverse)
    first_real = jnp.einsum('...ij,...jk,...kl->...il', factor_trans, middle, right_side, precision=high)
    first_imag = -jnp.einsum('...ij,...jk->...ik', factor_trans, right_side, precision=high)
    first = jnp.concatenate([first_real, first_imag], -1)
    first = 2.0 * first - complex_product(first, complex_product(matrix, first))
    return first

def from_below(stack, distance):
    return jnp.concatenate([jnp.zeros_like(stack[:distance]), stack[:-distance]], 0)

def from_above(stack, distance):
    return jnp.concatenate([stack[distance:], jnp.zeros_like(stack[:distance])], 0)

def reference(energy_sq, broadening, onsite, coupling, sigma_in, anharmonic, energy_pairs):
    slab_count = onsite.shape[0]
    block_width = onsite.shape[-1]
    identity = jnp.eye(block_width, dtype=jnp.float32)
    blank = jnp.zeros((slab_count, block_width, block_width), jnp.float32)
    bond_block = identity[None] + coupling
    bond_below = jnp.concatenate([jnp.zeros_like(bond_block[:1]), bond_block[:-1]], 0)
    upper_start = jnp.concatenate([-bond_block, blank], -1)
    lower_start = jnp.concatenate([-jnp.swapaxes(bond_below, 1, 2), blank], -1)

    def solve_energy(inputs):
        squared, damping, self_part = inputs
        diag_real = squared * identity[None] - onsite - self_part[..., :block_width]
        diag_imag = damping * identity[None] - self_part[..., block_width:]
        matrix = jnp.concatenate([diag_real, diag_imag], -1)
        lower_block = lower_start
        upper_block = upper_start
        distance = 1
        while distance < slab_count:
            inverse = invert(matrix)
            forward = complex_product(inverse, upper_block)
            backward = complex_product(inverse, lower_block)
            matrix = matrix - complex_product(lower_block, from_below(forward, distance)) - complex_product(upper_block, from_above(backward, distance))
            if 2 * distance < slab_count:
                new_lower = -complex_product(lower_block, from_below(backward, distance))
                new_upper = -complex_product(upper_block, from_above(forward, distance))
                lower_block = new_lower
                upper_block = new_upper
            distance = distance * 2
        return invert(matrix)
    green_diag = lax.map(solve_energy, (energy_sq, broadening, sigma_in))
    pair_count = energy_pairs.shape[1]
    scale = anharmonic / pair_count

    def target_sigma(index_table):

        def add_pair(carry, index_row):
            first = green_diag[index_row[0]]
            second = green_diag[index_row[1]]
            real_part = first[..., :block_width] * second[..., :block_width] - first[..., block_width:] * second[..., block_width:]
            imag_part = first[..., :block_width] * second[..., block_width:] + first[..., block_width:] * second[..., :block_width]
            return (carry + jnp.concatenate([real_part, imag_part], -1), None)
        summed, unused = lax.scan(add_pair, jnp.zeros((slab_count, block_width, 2 * block_width), jnp.float32), index_table)
        return jnp.concatenate([summed[..., :block_width] * scale, summed[..., block_width:] * scale], -1)
    sigma_out = lax.map(target_sigma, energy_pairs)
    return (green_diag, sigma_out)
```

```python
import jax
import jax.numpy as jnp
from jax import lax
from jax.experimental import pallas as pl
from jax.experimental.pallas import tpu as pltpu
from jax.sharding import PartitionSpec as P

HALF = 64
F32 = jnp.float32
BF16 = jnp.bfloat16


def iota(shape, axis):
    return lax.broadcasted_iota(jnp.int32, shape, axis)


def swap(x):
    tiles = [pltpu.roll(x[:, t : t + 128], HALF, 1) for t in range(0, x.shape[1], 128)]
    return tiles[0] if len(tiles) == 1 else jnp.concatenate(tiles, 1)


def times_i(x):
    turned = swap(x)
    return jnp.where((iota(turned.shape, 1) & (2 * HALF - 1)) < HALF, -turned, turned)


def split(x):
    high = x.astype(BF16)
    return high, (x - high.astype(F32)).astype(BF16)


def dot(a, b):
    return jnp.dot(a, b, preferred_element_type=F32)


def dot3(left, right):
    return dot(left[0], right[0]) + (dot(left[0], right[1]) + dot(left[1], right[0]))


def stack_rows(x):
    turned = times_i(x)
    parts = []
    for t in range(0, x.shape[0], HALF):
        parts += [x[t : t + HALF], turned[t : t + HALF]]
    return jnp.concatenate(parts, 0)


def product(left, right):
    return dot3(split(left), split(stack_rows(right)))


def join(parts):
    parts = [p for p in parts if p is not None]
    return jnp.concatenate(parts, 1)


def cut(x, start, stop):
    return x[:, start:stop] if stop > start else None


def row_of(x, s):
    return jnp.broadcast_to(x[s : s + 1, :], (8, 128))


def lane_of(x, k):
    return jnp.take_along_axis(x, jnp.full((8, 128), k, jnp.int32), axis=1)


def cmul(a, b):
    return (a[0] * b[0] - a[1] * b[1], a[0] * b[1] + a[1] * b[0])


def csub(a, b):
    return (a[0] - b[0], a[1] - b[1])


def cadd(a, b):
    return (a[0] + b[0], a[1] + b[1])


def scale_rows(z, u, su):
    return z[0] * u + z[1] * su, z[0] * su - z[1] * u


def invert_small(groups):
    lane = iota((8, 128), 1)
    sub = iota((8, 128), 0)
    sign = jnp.where(lane < HALF, -1.0, 1.0).astype(F32)
    groups = list(groups)
    for g0 in range(8):
        k = 8 * g0
        inside = ((lane & (HALF - 1)) >> 3) == g0
        cols = [(lane_of(groups[g0], k + j), lane_of(groups[g0], HALF + k + j)) for j in range(8)]
        row = groups[g0]
        srow = pltpu.roll(row, HALF, 1) * sign
        row = jnp.where(inside, jnp.where(lane - k == sub, 1.0, 0.0), row)
        srow = jnp.where(inside, jnp.where(lane - HALF - k == sub, 1.0, 0.0), srow)
        others = [
            None
            if g == g0
            else [(lane_of(groups[g], k + j), lane_of(groups[g], HALF + k + j)) for j in range(8)]
            for g in range(8)
        ]
        for i in (0, 2, 4, 6):
            left, right = cols[i], cols[i + 1]
            a = (row_of(left[0], i), row_of(left[1], i))
            c = (row_of(left[0], i + 1), row_of(left[1], i + 1))
            b = (row_of(right[0], i), row_of(right[1], i))
            d = (row_of(right[0], i + 1), row_of(right[1], i + 1))
            det = csub(cmul(a, d), cmul(b, c))
            r = 1.0 / (det[0] * det[0] + det[1] * det[1])
            over = (det[0] * r, -(det[1] * r))
            left = (left[0] - jnp.where(sub == i, 1.0, 0.0), left[1])
            right = (right[0] - jnp.where(sub == i + 1, 1.0, 0.0), right[1])
            for j in range(i + 2, 8):
                x = (row_of(cols[j][0], i), row_of(cols[j][1], i))
                y = (row_of(cols[j][0], i + 1), row_of(cols[j][1], i + 1))
                w1 = cmul(csub(cmul(d, x), cmul(b, y)), over)
                w2 = cmul(csub(cmul(a, y), cmul(c, x)), over)
                cols[j] = csub(cols[j], cadd(cmul(left, w1), cmul(right, w2)))
            x, sx, y, sy = row_of(row, i), row_of(srow, i), row_of(row, i + 1), row_of(srow, i + 1)
            dx, sdx = scale_rows(d, x, sx)
            by, sby = scale_rows(b, y, sy)
            ay, say = scale_rows(a, y, sy)
            cx, scx = scale_rows(c, x, sx)
            w1, sw1 = scale_rows(over, dx - by, sdx - sby)
            w2, sw2 = scale_rows(over, ay - cx, say - scx)
            u1, su1 = scale_rows(left, w1, sw1)
            u2, su2 = scale_rows(right, w2, sw2)
            row = row - (u1 + u2)
            srow = srow - (su1 + su2)
        rows = [(row_of(row, m), row_of(srow, m)) for m in range(8)]
        for g in range(8):
            if g == g0:
                groups[g] = row
                continue
            t = [others[g][m][0] * rows[m][0] + others[g][m][1] * rows[m][1] for m in range(8)]
            total = ((t[0] + t[1]) + (t[2] + t[3])) + ((t[4] + t[5]) + (t[6] + t[7]))
            groups[g] = jnp.where(inside, 0.0, groups[g]) - total
    return groups


def invert_in_place(a_ref):
    width = a_ref.shape[0]
    for k in range(0, width, HALF):
        t = 2 * k
        row = a_ref[k : k + HALF, :]
        turned = times_i(row)
        base = split(jnp.concatenate([jnp.concatenate([row, turned], 1), jnp.concatenate([turned, -row], 1)], 0))
        groups = [a_ref[k + 8 * g : k + 8 * g + 8, t : t + 128] for g in range(8)]
        inverse = jnp.concatenate(invert_small(groups), 0)
        both = dot3(split(inverse), base)
        n = 2 * width
        new_row = join([cut(both, 0, t), inverse, cut(both, t + 128, n)])
        new_turned = join([cut(both, n, n + t), times_i(inverse), cut(both, n + t + 128, 2 * n)])
        right = split(jnp.concatenate([new_row, new_turned], 0))
        for r in range(0, width, HALF):
            if r == k:
                continue
            keep = a_ref[r : r + HALF, :]
            left = split(keep[:, t : t + 128])
            keep = join([cut(keep, 0, t), jnp.zeros((HALF, 128), F32), cut(keep, t + 128, n)])
            a_ref[r : r + HALF, :] = keep - dot3(left, right)
        a_ref[k : k + HALF, :] = new_row


def to_tiles(x):
    low = iota((x.shape[0], 128), 1) < HALF
    t0, t1, t2 = x[:, :128], x[:, 128:256], x[:, 256:]
    middle = pltpu.roll(jnp.where(low, t2, t0), HALF, 1)
    return jnp.concatenate([jnp.where(low, t0, t1), middle, jnp.where(low, t1, t2)], 1)


def from_tiles(x):
    low = iota((x.shape[0], 128), 1) < HALF
    p0, p1, p2 = x[:, :128], x[:, 128:256], x[:, 256:]
    p1 = pltpu.roll(p1, HALF, 1)
    return jnp.concatenate([jnp.where(low, p0, p1), jnp.where(low, p2, p0), jnp.where(low, p1, p2)], 1)


def first_kernel(energy_ref, damping_ref, onsite_ref, sigma_ref, a_ref, x_ref, wide_ref):
    width = onsite_ref.shape[0]
    wide_ref[:, :width] = onsite_ref[...]
    low = iota((width, 128), 1) < HALF
    o0, o1 = wide_ref[:, :128], wide_ref[:, 128:]
    o0, om, o1 = (jnp.where(low, o, 0.0) for o in (o0, pltpu.roll(o0, HALF, 1), o1))
    row = iota((width, 3 * 128), 0)
    lane = iota((width, 3 * 128), 1)
    tile, inner = lane >> 7, lane & 127
    diag = jnp.where(
        row == tile * HALF + inner,
        jnp.where(inner < HALF, energy_ref[0], 0.0),
        jnp.where((row == tile * HALF + inner - HALF) & (inner >= HALF), damping_ref[0], 0.0),
    )
    diag = jnp.where((inner < HALF) | (row == tile * HALF + inner - HALF), diag, 0.0)
    a = diag - jnp.concatenate([o0, om, o1], 1) - to_tiles(sigma_ref[...])
    a_ref[...] = a
    x_ref[...] = a
    invert_in_place(x_ref)


def second_kernel(
    a_ref, below_ref, above_ref, left_b_ref, left_a_ref, right_b_ref, right_a_ref,
    a_out, l_out, u_out, p_out, x_ref,
):
    n = a_ref.shape[1]
    below = dot3(split(left_b_ref[...]), split(below_ref[...]))
    both = dot3(split(below), split(right_b_ref[...]))
    above = dot3(split(left_a_ref[...]), split(above_ref[...]))
    other = dot3(split(above), split(right_a_ref[...]))
    a = a_ref[...] - both[:, :n] - other[:, :n]
    lower = -both[:, n:]
    upper = -other[:, n:]
    a_out[...] = a
    l_out[...] = lower
    u_out[...] = upper
    x_ref[...] = a
    invert_in_place(x_ref)
    x = split(x_ref[...])
    p_out[0] = dot3(x, split(stack_rows(upper)))
    p_out[1] = dot3(x, split(stack_rows(lower)))


def middle_kernel(a_ref, l_ref, u_ref, below_ref, above_ref, a_out, l_out, u_out, p_out, x_ref):
    lower, upper = split(l_ref[...]), split(u_ref[...])
    a = a_ref[...] - dot3(lower, split(stack_rows(below_ref[0])))
    a = a - dot3(upper, split(stack_rows(above_ref[1])))
    new_lower = -dot3(lower, split(stack_rows(below_ref[1])))
    new_upper = -dot3(upper, split(stack_rows(above_ref[0])))
    a_out[...] = a
    l_out[...] = new_lower
    u_out[...] = new_upper
    x_ref[...] = a
    invert_in_place(x_ref)
    x = split(x_ref[...])
    p_out[0] = dot3(x, split(stack_rows(new_upper)))
    p_out[1] = dot3(x, split(stack_rows(new_lower)))


def pair_kernel(first_ref, a_ref, l_ref, u_ref, below_ref, above_ref, a_out, c_out, w_out, x_ref):
    first = first_ref[0] != 0
    a = a_ref[...] - product(l_ref[...], below_ref[0]) - product(u_ref[...], above_ref[1])
    left = jnp.where(first, u_ref[...], l_ref[...])
    right = jnp.where(first, above_ref[0], below_ref[1])
    link = -product(left, right)
    a_out[...] = a
    c_out[...] = link
    x_ref[...] = a
    invert_in_place(x_ref)
    w_out[...] = product(x_ref[...], link)


def last_kernel(a_ref, c_ref, w_ref, g_out, x_ref):
    x_ref[...] = a_ref[...] - product(c_ref[...], w_ref[...])
    invert_in_place(x_ref)
    g_out[...] = from_tiles(x_ref[...])


def sigma_kernel(pairs_ref, scale_ref, *refs):
    green, out_ref, wide_ref = refs[:-2], refs[-2], refs[-1]
    count = len(green)
    pair_count = pairs_ref.shape[0]
    width = scale_ref.shape[0]
    weight = {}
    for i in range(count):
        for j in range(i, count):
            total = jnp.int32(0)
            for p in range(pair_count):
                e1, e2 = pairs_ref[p, 0], pairs_ref[p, 1]
                hit = ((e1 == i) & (e2 == j)) | ((e1 == j) & (e2 == i))
                total = total + hit.astype(jnp.int32)
            weight[i, j] = total.astype(F32)
    wide_ref[:, :width] = scale_ref[...] * (1.0 / pair_count)
    low = iota((8, 128), 1) < HALF

    def step(r, carry):
        here = pl.ds(pl.multiple_of(8 * r, 8), 8)
        main, rest = [], []
        for g in green:
            t0, t1, t2 = g[here, :128], g[here, 128:256], g[here, 256:]
            main.append((t0, pltpu.roll(jnp.where(low, t2, t1), HALF, 1)))
            rest.append((t1, pltpu.roll(t2, HALF, 1)))

        def combine(z):
            total = None
            for i in range(count):
                inner = None
                for j in range(i, count):
                    term = (weight[i, j] * z[j][0], weight[i, j] * z[j][1])
                    inner = term if inner is None else cadd(inner, term)
                term = cmul(z[i], inner)
                total = term if total is None else cadd(total, term)
            return total

        s0, s1 = wide_ref[here, :128], wide_ref[here, 128:]
        m = combine(main)
        q = combine(rest)
        mr, mi = m[0] * s0, m[1] * s0
        qr, qi = q[0] * s1, q[1] * s1
        mi = pltpu.roll(mi, HALF, 1)
        qi = pltpu.roll(qi, HALF, 1)
        out_ref[here, :128] = mr
        out_ref[here, 128:256] = jnp.where(low, qr, mi)
        out_ref[here, 256:] = jnp.where(low, mi, qi)
        return carry

    lax.fori_loop(0, width // 8, step, 0)


def call(kernel, ins, outs, scratch=(), scalars=0):
    vmem = pl.BlockSpec(memory_space=pltpu.VMEM)
    smem = pl.BlockSpec(memory_space=pltpu.SMEM)
    return pl.pallas_call(
        kernel,
        out_shape=tuple(jax.ShapeDtypeStruct(s, F32) for s in outs),
        in_specs=[smem] * scalars + [vmem] * (len(ins) - scalars),
        out_specs=tuple(vmem for _ in outs),
        scratch_shapes=[pltpu.VMEM(s, F32) for s in scratch],
        compiler_params=pltpu.CompilerParams(vmem_limit_bytes=56 * 2**20),
    )(*ins)


def shifted(value, axis, steps):
    count = lax.axis_size(axis)
    first, last = max(0, -steps), min(count, count - steps)
    return lax.ppermute(value, axis, [(source, source + steps) for source in range(first, last)])


def spread(real):
    width = real.shape[0]
    t = width // HALF
    blocks = real.reshape(t, 1, HALF, t, 1, HALF)
    keep = jnp.eye(2, dtype=F32).reshape(1, 2, 1, 1, 2, 1)
    return (blocks * keep).reshape(2 * width, 2 * width)


def shards(energy_sq, broadening, onsite, coupling, sigma_in, anharmonic, energy_pairs):
    width = onsite.shape[-1]
    block = (width, 2 * width)
    count = lax.axis_size("slab")
    level_count = count.bit_length() - 1
    slab = lax.axis_index("slab")
    identity = jnp.eye(width, dtype=F32)
    here = coupling[0]
    below1 = shifted(here, "slab", 1)
    below2 = shifted(here, "slab", 2)
    above1 = shifted(here, "slab", -1)

    a, x0 = call(
        first_kernel, (energy_sq, broadening, onsite[0], sigma_in[0, 0]), (block, block),
        scratch=((width, 256),), scalars=2,
    )
    x_below = shifted(x0, "slab", 1)
    x_above = shifted(x0, "slab", -1)
    bond = identity + here
    bond_below = identity + below1
    bond_below2 = jnp.where(slab >= 2, 1.0, 0.0) * (identity + below2)
    bond_above = identity + above1
    right_below = jnp.concatenate([spread(bond_below), spread(bond_below2.T)], 1)
    right_above = jnp.concatenate([spread(bond.T), spread(bond_above)], 1)
    a, lower, upper, payload = call(
        second_kernel,
        (a, x_below, x_above, bond_below.T, bond, right_below, right_above),
        (block, block, block, (2,) + block),
        scratch=(block,),
    )
    for level in range(1, level_count - 1):
        below = shifted(payload, "slab", 2**level)
        above = shifted(payload, "slab", -(2**level))
        if level < level_count - 2:
            a, lower, upper, payload = call(
                middle_kernel, (a, lower, upper, below, above),
                (block, block, block, (2,) + block), scratch=(block,),
            )
    half = count // 2
    first = (slab < half).astype(jnp.int32).reshape(1)
    a, link, w = call(
        pair_kernel, (first, a, lower, upper, below, above), (block, block, block),
        scratch=(block,), scalars=1,
    )
    w = lax.ppermute(w, "slab", [(s, s ^ half) for s in range(count)])
    (green,) = call(last_kernel, (a, link, w), (block,), scratch=(block,))

    energies = lax.axis_size("energy")
    everyone = green[None]
    step = energies // 2
    order = [0]
    while step:
        other = lax.ppermute(everyone, "energy", [(e, e ^ step) for e in range(energies)])
        everyone = jnp.concatenate([everyone, other], 0) if step > 1 else (everyone, other)
        order = order + [o ^ step for o in order]
        step //= 2
    blocks = [e[i] for e in everyone for i in range(e.shape[0])]
    table = [blocks[order.index(o)] for o in range(energies)]
    (sigma,) = call(
        sigma_kernel, (energy_pairs[0] ^ lax.axis_index("energy"), anharmonic[0], *table), (block,),
        scratch=((width, 256),), scalars=1,
    )
    return green[None, None], sigma[None, None]


def solution(mesh):
    in_specs = (
        P("energy"),
        P("energy"),
        P("slab", None, None),
        P("slab", None, None),
        P("energy", "slab", None, None),
        P("slab", None, None),
        P("energy", None, None),
    )
    out_specs = (P("energy", "slab", None, None), P("energy", "slab", None, None))
    return jax.shard_map(shards, mesh=mesh, in_specs=in_specs, out_specs=out_specs, check_vma=False)
```

```python
import functools

import jax
import jax.numpy as jnp
from jax import lax
from jax.experimental import pallas as pl
from jax.experimental.pallas import tpu as pltpu
from jax.sharding import PartitionSpec as P

HALF = 64
F32 = jnp.float32
BF16 = jnp.bfloat16


def iota(shape, axis):
    return lax.broadcasted_iota(jnp.int32, shape, axis)


def swap(x):
    tiles = [pltpu.roll(x[:, t : t + 128], HALF, 1) for t in range(0, x.shape[1], 128)]
    return tiles[0] if len(tiles) == 1 else jnp.concatenate(tiles, 1)


def times_i(x):
    turned = swap(x)
    return jnp.where((iota(turned.shape, 1) & (2 * HALF - 1)) < HALF, -turned, turned)


def split(x):
    high = x.astype(BF16)
    return high, (x - high.astype(F32)).astype(BF16)


def dot(a, b):
    return jnp.dot(a, b, preferred_element_type=F32)


def dot3(left, right):
    return dot(left[0], right[0]) + (dot(left[0], right[1]) + dot(left[1], right[0]))


def stack_rows(x):
    turned = times_i(x)
    parts = []
    for t in range(0, x.shape[0], HALF):
        parts += [x[t : t + HALF], turned[t : t + HALF]]
    return jnp.concatenate(parts, 0)


def product(left, right):
    return dot3(split(left), split(stack_rows(right)))


def join(parts):
    parts = [p for p in parts if p is not None]
    return jnp.concatenate(parts, 1)


def cut(x, start, stop):
    return x[:, start:stop] if stop > start else None


def row_of(x, s):
    return jnp.broadcast_to(x[s : s + 1, :], (8, 128))


def lane_of(x, k):
    return jnp.take_along_axis(x, jnp.full((8, 128), k, jnp.int32), axis=1)


def cmul(a, b):
    return (a[0] * b[0] - a[1] * b[1], a[0] * b[1] + a[1] * b[0])


def csub(a, b):
    return (a[0] - b[0], a[1] - b[1])


def cadd(a, b):
    return (a[0] + b[0], a[1] + b[1])


def scale_rows(z, u, su):
    return z[0] * u + z[1] * su, z[0] * su - z[1] * u


def invert_small(groups):
    lane = iota((8, 128), 1)
    sub = iota((8, 128), 0)
    sign = jnp.where(lane < HALF, -1.0, 1.0).astype(F32)
    groups = list(groups)
    for g0 in range(8):
        k = 8 * g0
        inside = ((lane & (HALF - 1)) >> 3) == g0
        cols = [(lane_of(groups[g0], k + j), lane_of(groups[g0], HALF + k + j)) for j in range(8)]
        row = groups[g0]
        srow = pltpu.roll(row, HALF, 1) * sign
        row = jnp.where(inside, jnp.where(lane - k == sub, 1.0, 0.0), row)
        srow = jnp.where(inside, jnp.where(lane - HALF - k == sub, 1.0, 0.0), srow)
        others = [
            None
            if g == g0
            else [(lane_of(groups[g], k + j), lane_of(groups[g], HALF + k + j)) for j in range(8)]
            for g in range(8)
        ]
        for i in (0, 2, 4, 6):
            left, right = cols[i], cols[i + 1]
            a = (row_of(left[0], i), row_of(left[1], i))
            c = (row_of(left[0], i + 1), row_of(left[1], i + 1))
            b = (row_of(right[0], i), row_of(right[1], i))
            d = (row_of(right[0], i + 1), row_of(right[1], i + 1))
            det = csub(cmul(a, d), cmul(b, c))
            r = 1.0 / (det[0] * det[0] + det[1] * det[1])
            over = (det[0] * r, -(det[1] * r))
            left = (left[0] - jnp.where(sub == i, 1.0, 0.0), left[1])
            right = (right[0] - jnp.where(sub == i + 1, 1.0, 0.0), right[1])
            for j in range(i + 2, 8):
                x = (row_of(cols[j][0], i), row_of(cols[j][1], i))
                y = (row_of(cols[j][0], i + 1), row_of(cols[j][1], i + 1))
                w1 = cmul(csub(cmul(d, x), cmul(b, y)), over)
                w2 = cmul(csub(cmul(a, y), cmul(c, x)), over)
                cols[j] = csub(cols[j], cadd(cmul(left, w1), cmul(right, w2)))
            x, sx, y, sy = row_of(row, i), row_of(srow, i), row_of(row, i + 1), row_of(srow, i + 1)
            dx, sdx = scale_rows(d, x, sx)
            by, sby = scale_rows(b, y, sy)
            ay, say = scale_rows(a, y, sy)
            cx, scx = scale_rows(c, x, sx)
            w1, sw1 = scale_rows(over, dx - by, sdx - sby)
            w2, sw2 = scale_rows(over, ay - cx, say - scx)
            u1, su1 = scale_rows(left, w1, sw1)
            u2, su2 = scale_rows(right, w2, sw2)
            row = row - (u1 + u2)
            srow = srow - (su1 + su2)
        rows = [(row_of(row, m), row_of(srow, m)) for m in range(8)]
        for g in range(8):
            if g == g0:
                groups[g] = row
                continue
            t = [others[g][m][0] * rows[m][0] + others[g][m][1] * rows[m][1] for m in range(8)]
            total = ((t[0] + t[1]) + (t[2] + t[3])) + ((t[4] + t[5]) + (t[6] + t[7]))
            groups[g] = jnp.where(inside, 0.0, groups[g]) - total
    return groups


def invert_in_place(a_ref):
    width = a_ref.shape[0]
    for k in range(0, width, HALF):
        t = 2 * k
        row = a_ref[k : k + HALF, :]
        turned = times_i(row)
        base = split(jnp.concatenate([jnp.concatenate([row, turned], 1), jnp.concatenate([turned, -row], 1)], 0))
        groups = [a_ref[k + 8 * g : k + 8 * g + 8, t : t + 128] for g in range(8)]
        inverse = jnp.concatenate(invert_small(groups), 0)
        both = dot3(split(inverse), base)
        n = 2 * width
        new_row = join([cut(both, 0, t), inverse, cut(both, t + 128, n)])
        new_turned = join([cut(both, n, n + t), times_i(inverse), cut(both, n + t + 128, 2 * n)])
        right = split(jnp.concatenate([new_row, new_turned], 0))
        for r in range(0, width, HALF):
            if r == k:
                continue
            keep = a_ref[r : r + HALF, :]
            left = split(keep[:, t : t + 128])
            keep = join([cut(keep, 0, t), jnp.zeros((HALF, 128), F32), cut(keep, t + 128, n)])
            a_ref[r : r + HALF, :] = keep - dot3(left, right)
        a_ref[k : k + HALF, :] = new_row


def to_tiles(x):
    low = iota((x.shape[0], 128), 1) < HALF
    t0, t1, t2 = x[:, :128], x[:, 128:256], x[:, 256:]
    middle = pltpu.roll(jnp.where(low, t2, t0), HALF, 1)
    return jnp.concatenate([jnp.where(low, t0, t1), middle, jnp.where(low, t1, t2)], 1)


def from_tiles(x):
    low = iota((x.shape[0], 128), 1) < HALF
    p0, p1, p2 = x[:, :128], x[:, 128:256], x[:, 256:]
    p1 = pltpu.roll(p1, HALF, 1)
    return jnp.concatenate([jnp.where(low, p0, p1), jnp.where(low, p2, p0), jnp.where(low, p1, p2)], 1)


def first_kernel(energy_ref, damping_ref, onsite_ref, sigma_ref, a_ref, x_ref, wide_ref):
    width = onsite_ref.shape[0]
    wide_ref[:, :width] = onsite_ref[...]
    low = iota((width, 128), 1) < HALF
    o0, o1 = wide_ref[:, :128], wide_ref[:, 128:]
    o0, om, o1 = (jnp.where(low, o, 0.0) for o in (o0, pltpu.roll(o0, HALF, 1), o1))
    row = iota((width, 3 * 128), 0)
    lane = iota((width, 3 * 128), 1)
    tile, inner = lane >> 7, lane & 127
    diag = jnp.where(
        row == tile * HALF + inner,
        jnp.where(inner < HALF, energy_ref[0], 0.0),
        jnp.where((row == tile * HALF + inner - HALF) & (inner >= HALF), damping_ref[0], 0.0),
    )
    diag = jnp.where((inner < HALF) | (row == tile * HALF + inner - HALF), diag, 0.0)
    a = diag - jnp.concatenate([o0, om, o1], 1) - to_tiles(sigma_ref[...])
    a_ref[...] = a
    x_ref[...] = a
    invert_in_place(x_ref)


def real_tiles(x, wide_ref):
    width = x.shape[0]
    wide_ref[:, :width] = x
    low = iota((width, 128), 1) < HALF
    o0, o1 = wide_ref[:, :128], wide_ref[:, 128:]
    return jnp.concatenate([jnp.where(low, o, 0.0) for o in (o0, pltpu.roll(o0, HALF, 1), o1)], 1)


def put(out_ref, pair, columns=slice(None)):
    out_ref[0, :, columns] = pair[0]
    out_ref[1, :, columns] = pair[1]


def prepare_kernel(
    energies, slab_ref, pairs_ref, here_ref, swap_a_ref, swap_b_ref, below2_ref,
    left_b_out, left_a_out, right_b_out, right_a_out, weight_out, wide_ref,
):
    width = here_ref.shape[0]
    slab = slab_ref[0]
    odd = (slab & 1) == 1
    eye = jnp.where(iota((width, width), 0) == iota((width, width), 1), 1.0, 0.0)
    a, b = swap_a_ref[...], swap_b_ref[...]
    here = eye + here_ref[...]
    below = eye + jnp.where(odd, a, b)
    above = eye + jnp.where(odd, b, a)
    below2 = jnp.where(slab >= 2, eye + below2_ref[...], 0.0)
    put(left_b_out, split(below.T))
    put(left_a_out, split(here))
    for columns, out, block in (
        (slice(0, 2 * width), right_b_out, below),
        (slice(2 * width, 4 * width), right_b_out, below2.T),
        (slice(0, 2 * width), right_a_out, here.T),
        (slice(2 * width, 4 * width), right_a_out, above),
    ):
        put(out, split(stack_rows(real_tiles(block, wide_ref))), columns)
    count = slab_ref[1]
    for i in range(energies):
        for j in range(i, energies):
            total = jnp.int32(0)
            for p in range(pairs_ref.shape[0]):
                e1, e2 = pairs_ref[p, 0] ^ count, pairs_ref[p, 1] ^ count
                hit = ((e1 == i) & (e2 == j)) | ((e1 == j) & (e2 == i))
                total = total + hit.astype(jnp.int32)
            weight_out[energies * i + j] = jnp.full((8, 128), total.astype(F32))


def pair(ref):
    return ref[0], ref[1]


def second_kernel(
    slab_ref, a_ref, swap_a_ref, swap_b_ref, left_b_ref, left_a_ref, right_b_ref, right_a_ref,
    a_out, l_out, u_out, p_out, x_ref,
):
    n = a_ref.shape[1]
    odd = (slab_ref[0] & 1) == 1
    swap_a, swap_b = swap_a_ref[...], swap_b_ref[...]
    below = dot3(pair(left_b_ref), split(jnp.where(odd, swap_a, swap_b)))
    both = dot3(split(below), pair(right_b_ref))
    above = dot3(pair(left_a_ref), split(jnp.where(odd, swap_b, swap_a)))
    other = dot3(split(above), pair(right_a_ref))
    a = a_ref[...] - both[:, :n] - other[:, :n]
    lower = -both[:, n:]
    upper = -other[:, n:]
    a_out[...] = a
    l_out[...] = lower
    u_out[...] = upper
    x_ref[...] = a
    invert_in_place(x_ref)
    x = split(x_ref[...])
    p_out[0] = dot3(x, split(stack_rows(upper)))
    p_out[1] = dot3(x, split(stack_rows(lower)))


def sides(slab_ref, distance, swap_a_ref, swap_b_ref, i, j):
    low = (slab_ref[0] & distance) == 0
    below = jnp.where(low, swap_b_ref[i], swap_a_ref[i])
    above = jnp.where(low, swap_a_ref[j], swap_b_ref[j])
    return below, above


def middle_kernel(distance, slab_ref, a_ref, l_ref, u_ref, swap_a_ref, swap_b_ref, a_out, l_out, u_out, p_out, x_ref):
    lower, upper = split(l_ref[...]), split(u_ref[...])
    forward, backward = sides(slab_ref, distance, swap_a_ref, swap_b_ref, 0, 1)
    a = a_ref[...] - dot3(lower, split(stack_rows(forward)))
    a = a - dot3(upper, split(stack_rows(backward)))
    backward, forward = sides(slab_ref, distance, swap_a_ref, swap_b_ref, 1, 0)
    new_lower = -dot3(lower, split(stack_rows(backward)))
    new_upper = -dot3(upper, split(stack_rows(forward)))
    a_out[...] = a
    l_out[...] = new_lower
    u_out[...] = new_upper
    x_ref[...] = a
    invert_in_place(x_ref)
    x = split(x_ref[...])
    p_out[0] = dot3(x, split(stack_rows(new_upper)))
    p_out[1] = dot3(x, split(stack_rows(new_lower)))


def pair_kernel(distance, half, slab_ref, a_ref, l_ref, u_ref, swap_a_ref, swap_b_ref, a_out, c_out, w_out, x_ref):
    first = slab_ref[0] < half
    forward, backward = sides(slab_ref, distance, swap_a_ref, swap_b_ref, 0, 1)
    a = a_ref[...] - product(l_ref[...], forward) - product(u_ref[...], backward)
    backward, forward = sides(slab_ref, distance, swap_a_ref, swap_b_ref, 1, 0)
    left = jnp.where(first, u_ref[...], l_ref[...])
    link = -product(left, jnp.where(first, forward, backward))
    a_out[...] = a
    c_out[...] = link
    x_ref[...] = a
    invert_in_place(x_ref)
    w_out[...] = product(x_ref[...], link)


def last_kernel(a_ref, c_ref, w_ref, g_out, x_ref):
    x_ref[...] = a_ref[...] - product(c_ref[...], w_ref[...])
    invert_in_place(x_ref)
    g_out[...] = from_tiles(x_ref[...])


def sigma_kernel(pair_count, weight_ref, scale_ref, *refs):
    green, out_ref, wide_ref = refs[:-2], refs[-2], refs[-1]
    count = len(green)
    width = scale_ref.shape[0]
    wide_ref[:, :width] = scale_ref[...] * (1.0 / pair_count)
    rows = HALF
    low = iota((rows, 128), 1) < HALF

    def weight(i, j):
        return jnp.broadcast_to(weight_ref[count * i + j, :1, :], (rows, 128))

    def combine(z):
        total = None
        for i in range(count):
            inner = None
            for j in range(i, count):
                w = weight(i, j)
                term = (w * z[j][0], w * z[j][1])
                inner = term if inner is None else cadd(inner, term)
            term = cmul(z[i], inner)
            total = term if total is None else cadd(total, term)
        return total

    for r in range(0, width, rows):
        here = slice(r, r + rows)
        main, rest = [], []
        for g in green:
            t0, t1, t2 = g[here, :128], g[here, 128:256], g[here, 256:]
            main.append((t0, pltpu.roll(jnp.where(low, t2, t1), HALF, 1)))
            rest.append((t1, pltpu.roll(t2, HALF, 1)))
        s0, s1 = wide_ref[here, :128], wide_ref[here, 128:]
        m = combine(main)
        q = combine(rest)
        mi = pltpu.roll(m[1] * s0, HALF, 1)
        qi = pltpu.roll(q[1] * s1, HALF, 1)
        out_ref[here, :128] = m[0] * s0
        out_ref[here, 128:256] = jnp.where(low, q[0] * s1, mi)
        out_ref[here, 256:] = jnp.where(low, mi, qi)


def call(kernel, ins, outs, scratch=(), scalars=0):
    vmem = pl.BlockSpec(memory_space=pltpu.VMEM)
    smem = pl.BlockSpec(memory_space=pltpu.SMEM)
    outs = tuple(o if isinstance(o, jax.ShapeDtypeStruct) else jax.ShapeDtypeStruct(o, F32) for o in outs)
    return pl.pallas_call(
        kernel,
        out_shape=outs,
        in_specs=[smem] * scalars + [vmem] * (len(ins) - scalars),
        out_specs=tuple(vmem for _ in outs),
        scratch_shapes=[pltpu.VMEM(s, F32) for s in scratch],
        compiler_params=pltpu.CompilerParams(vmem_limit_bytes=56 * 2**20),
    )(*ins)


def swaps(value, distance):
    count = lax.axis_size("slab")
    near = [(s, s ^ distance) for s in range(count)]
    far = [(s, s + distance if s & distance else s - distance) for s in range(count)]
    far = [(s, t) for s, t in far if 0 <= t < count]
    return lax.ppermute(value, "slab", near), lax.ppermute(value, "slab", far)


def shards(energy_sq, broadening, onsite, coupling, sigma_in, anharmonic, energy_pairs):
    width = onsite.shape[-1]
    block = (width, 2 * width)
    count = lax.axis_size("slab")
    energies = lax.axis_size("energy")
    level_count = count.bit_length() - 1
    slab = lax.axis_index("slab").astype(jnp.int32)
    place = jnp.stack([slab, lax.axis_index("energy").astype(jnp.int32)])
    here = coupling[0]
    bond_a, bond_b = swaps(here, 1)
    a, x0 = call(
        first_kernel, (energy_sq, broadening, onsite[0], sigma_in[0, 0]), (block, block),
        scratch=((width, 256),), scalars=2,
    )
    swap_a, swap_b = swaps(x0, 1)
    here, x0 = lax.optimization_barrier((here, x0))
    below2 = lax.ppermute(here, "slab", [(s, s + 2) for s in range(count - 2)])
    wide = jax.ShapeDtypeStruct((2, 2 * width, 4 * width), BF16)
    real = jax.ShapeDtypeStruct((2, width, width), BF16)
    *operands, weight = call(
        functools.partial(prepare_kernel, energies), (place, energy_pairs[0], here, bond_a, bond_b, below2),
        (real, real, wide, wide, (energies**2, 8, 128)), scratch=((width, 256),), scalars=2,
    )
    a, lower, upper, payload = call(
        second_kernel, (place, a, swap_a, swap_b, *operands),
        (block, block, block, (2,) + block), scratch=(block,), scalars=1,
    )
    for level in range(1, level_count - 1):
        distance = 2**level
        swap_a, swap_b = swaps(payload, distance)
        if level < level_count - 2:
            a, lower, upper, payload = call(
                functools.partial(middle_kernel, distance), (place, a, lower, upper, swap_a, swap_b),
                (block, block, block, (2,) + block), scratch=(block,), scalars=1,
            )
    half = count // 2
    a, link, w = call(
        functools.partial(pair_kernel, half // 2, half), (place, a, lower, upper, swap_a, swap_b),
        (block, block, block), scratch=(block,), scalars=1,
    )
    w = lax.ppermute(w, "slab", [(s, s ^ half) for s in range(count)])
    (green,) = call(last_kernel, (a, link, w), (block,), scratch=(block,))

    table = {0: green}
    step = energies // 2
    while step:
        for offset in list(table):
            table[offset ^ step] = lax.ppermute(
                table[offset], "energy", [(e, e ^ step) for e in range(energies)]
            )
        step //= 2
    (sigma,) = call(
        functools.partial(sigma_kernel, energy_pairs.shape[1]),
        (weight, anharmonic[0], *(table[o] for o in range(energies))), (block,), scratch=((width, 256),),
    )
    return green[None, None], sigma[None, None]


def solution(mesh):
    in_specs = (
        P("energy"),
        P("energy"),
        P("slab", None, None),
        P("slab", None, None),
        P("energy", "slab", None, None),
        P("slab", None, None),
        P("energy", None, None),
    )
    out_specs = (P("energy", "slab", None, None), P("energy", "slab", None, None))
    return jax.shard_map(shards, mesh=mesh, in_specs=in_specs, out_specs=out_specs, check_vma=False)
```

```python
import functools

import jax
import jax.numpy as jnp
from jax import lax
from jax.experimental import pallas as pl
from jax.experimental.pallas import tpu as pltpu
from jax.sharding import PartitionSpec as P


HALF = 64
F32 = jnp.float32
BF16 = jnp.bfloat16


def iota(shape, axis):
    return lax.broadcasted_iota(jnp.int32, shape, axis)


def swap(x):
    tiles = [pltpu.roll(x[:, t : t + 128], HALF, 1) for t in range(0, x.shape[1], 128)]
    return tiles[0] if len(tiles) == 1 else jnp.concatenate(tiles, 1)


def times_i(x):
    turned = swap(x)
    return jnp.where((iota(turned.shape, 1) & (2 * HALF - 1)) < HALF, -turned, turned)


def split(x):
    high = x.astype(BF16)
    return high, (x - high.astype(F32)).astype(BF16)


def dot(a, b):
    return jnp.dot(a, b, preferred_element_type=F32)


def dot3(left, right):
    return dot(left[0], right[0]) + (dot(left[0], right[1]) + dot(left[1], right[0]))


def stack_rows(x):
    turned = times_i(x)
    parts = []
    for t in range(0, x.shape[0], HALF):
        parts += [x[t : t + HALF], turned[t : t + HALF]]
    return jnp.concatenate(parts, 0)


def product(left, right):
    return dot3(split(left), split(stack_rows(right)))


def join(parts):
    parts = [p for p in parts if p is not None]
    return jnp.concatenate(parts, 1)


def cut(x, start, stop):
    return x[:, start:stop] if stop > start else None


def row_of(x, s):
    return jnp.broadcast_to(x[s : s + 1, :], (8, 128))


def lane_of(x, k):
    return jnp.take_along_axis(x, jnp.full((8, 128), k, jnp.int32), axis=1)


def cmul(a, b):
    return (a[0] * b[0] - a[1] * b[1], a[0] * b[1] + a[1] * b[0])


def csub(a, b):
    return (a[0] - b[0], a[1] - b[1])


def cadd(a, b):
    return (a[0] + b[0], a[1] + b[1])


def scale_rows(z, u, su):
    return z[0] * u + z[1] * su, z[0] * su - z[1] * u


def invert_small(groups):
    lane = iota((8, 128), 1)
    sub = iota((8, 128), 0)
    sign = jnp.where(lane < HALF, -1.0, 1.0).astype(F32)
    groups = list(groups)
    for g0 in range(8):
        k = 8 * g0
        inside = ((lane & (HALF - 1)) >> 3) == g0
        cols = [(lane_of(groups[g0], k + j), lane_of(groups[g0], HALF + k + j)) for j in range(8)]
        row = groups[g0]
        srow = pltpu.roll(row, HALF, 1) * sign
        row = jnp.where(inside, jnp.where(lane - k == sub, 1.0, 0.0), row)
        srow = jnp.where(inside, jnp.where(lane - HALF - k == sub, 1.0, 0.0), srow)
        others = [
            None
            if g == g0
            else [(lane_of(groups[g], k + j), lane_of(groups[g], HALF + k + j)) for j in range(8)]
            for g in range(8)
        ]
        for i in (0, 2, 4, 6):
            left, right = cols[i], cols[i + 1]
            a = (row_of(left[0], i), row_of(left[1], i))
            c = (row_of(left[0], i + 1), row_of(left[1], i + 1))
            b = (row_of(right[0], i), row_of(right[1], i))
            d = (row_of(right[0], i + 1), row_of(right[1], i + 1))
            det = csub(cmul(a, d), cmul(b, c))
            r = 1.0 / (det[0] * det[0] + det[1] * det[1])
            over = (det[0] * r, -(det[1] * r))
            left = (left[0] - jnp.where(sub == i, 1.0, 0.0), left[1])
            right = (right[0] - jnp.where(sub == i + 1, 1.0, 0.0), right[1])
            for j in range(i + 2, 8):
                x = (row_of(cols[j][0], i), row_of(cols[j][1], i))
                y = (row_of(cols[j][0], i + 1), row_of(cols[j][1], i + 1))
                w1 = cmul(csub(cmul(d, x), cmul(b, y)), over)
                w2 = cmul(csub(cmul(a, y), cmul(c, x)), over)
                cols[j] = csub(cols[j], cadd(cmul(left, w1), cmul(right, w2)))
            x, sx, y, sy = row_of(row, i), row_of(srow, i), row_of(row, i + 1), row_of(srow, i + 1)
            dx, sdx = scale_rows(d, x, sx)
            by, sby = scale_rows(b, y, sy)
            ay, say = scale_rows(a, y, sy)
            cx, scx = scale_rows(c, x, sx)
            w1, sw1 = scale_rows(over, dx - by, sdx - sby)
            w2, sw2 = scale_rows(over, ay - cx, say - scx)
            u1, su1 = scale_rows(left, w1, sw1)
            u2, su2 = scale_rows(right, w2, sw2)
            row = row - (u1 + u2)
            srow = srow - (su1 + su2)
        rows = [(row_of(row, m), row_of(srow, m)) for m in range(8)]
        for g in range(8):
            if g == g0:
                groups[g] = row
                continue
            t = [others[g][m][0] * rows[m][0] + others[g][m][1] * rows[m][1] for m in range(8)]
            total = ((t[0] + t[1]) + (t[2] + t[3])) + ((t[4] + t[5]) + (t[6] + t[7]))
            groups[g] = jnp.where(inside, 0.0, groups[g]) - total
    return groups


def invert_in_place(a_ref):
    width = a_ref.shape[0]
    for k in range(0, width, HALF):
        t = 2 * k
        row = a_ref[k : k + HALF, :]
        turned = times_i(row)
        base = split(jnp.concatenate([jnp.concatenate([row, turned], 1), jnp.concatenate([turned, -row], 1)], 0))
        groups = [a_ref[k + 8 * g : k + 8 * g + 8, t : t + 128] for g in range(8)]
        inverse = jnp.concatenate(invert_small(groups), 0)
        both = dot3(split(inverse), base)
        n = 2 * width
        new_row = join([cut(both, 0, t), inverse, cut(both, t + 128, n)])
        new_turned = join([cut(both, n, n + t), times_i(inverse), cut(both, n + t + 128, 2 * n)])
        right = split(jnp.concatenate([new_row, new_turned], 0))
        for r in range(0, width, HALF):
            if r == k:
                continue
            keep = a_ref[r : r + HALF, :]
            left = split(keep[:, t : t + 128])
            keep = join([cut(keep, 0, t), jnp.zeros((HALF, 128), F32), cut(keep, t + 128, n)])
            a_ref[r : r + HALF, :] = keep - dot3(left, right)
        a_ref[k : k + HALF, :] = new_row


def to_tiles(x):
    low = iota((x.shape[0], 128), 1) < HALF
    t0, t1, t2 = x[:, :128], x[:, 128:256], x[:, 256:]
    middle = pltpu.roll(jnp.where(low, t2, t0), HALF, 1)
    return jnp.concatenate([jnp.where(low, t0, t1), middle, jnp.where(low, t1, t2)], 1)


def from_tiles(x):
    low = iota((x.shape[0], 128), 1) < HALF
    p0, p1, p2 = x[:, :128], x[:, 128:256], x[:, 256:]
    p1 = pltpu.roll(p1, HALF, 1)
    return jnp.concatenate([jnp.where(low, p0, p1), jnp.where(low, p2, p0), jnp.where(low, p1, p2)], 1)


def first_kernel(energy_ref, damping_ref, onsite_ref, sigma_ref, a_ref, x_ref, wide_ref):
    width = onsite_ref.shape[0]
    wide_ref[:, :width] = onsite_ref[...]
    low = iota((width, 128), 1) < HALF
    o0, o1 = wide_ref[:, :128], wide_ref[:, 128:]
    o0, om, o1 = (jnp.where(low, o, 0.0) for o in (o0, pltpu.roll(o0, HALF, 1), o1))
    row = iota((width, 3 * 128), 0)
    lane = iota((width, 3 * 128), 1)
    tile, inner = lane >> 7, lane & 127
    diag = jnp.where(
        row == tile * HALF + inner,
        jnp.where(inner < HALF, energy_ref[0], 0.0),
        jnp.where((row == tile * HALF + inner - HALF) & (inner >= HALF), damping_ref[0], 0.0),
    )
    diag = jnp.where((inner < HALF) | (row == tile * HALF + inner - HALF), diag, 0.0)
    a = diag - jnp.concatenate([o0, om, o1], 1) - to_tiles(sigma_ref[...])
    a_ref[...] = a
    x_ref[...] = a
    invert_in_place(x_ref)


def real_tiles(x, wide_ref):
    width = x.shape[0]
    wide_ref[:, :width] = x
    low = iota((width, 128), 1) < HALF
    o0, o1 = wide_ref[:, :128], wide_ref[:, 128:]
    return jnp.concatenate([jnp.where(low, o, 0.0) for o in (o0, pltpu.roll(o0, HALF, 1), o1)], 1)


def put(out_ref, pair, columns=slice(None)):
    out_ref[0, :, columns] = pair[0]
    out_ref[1, :, columns] = pair[1]


def prepare_kernel(
    energies, slab_ref, pairs_ref, here_ref, swap_a_ref, swap_b_ref, below2_ref,
    left_b_out, left_a_out, right_b_out, right_a_out, weight_out, wide_ref,
):
    width = here_ref.shape[0]
    slab = slab_ref[0]
    odd = (slab & 1) == 1
    eye = jnp.where(iota((width, width), 0) == iota((width, width), 1), 1.0, 0.0)
    a, b = swap_a_ref[...], swap_b_ref[...]
    here = eye + here_ref[...]
    below = eye + jnp.where(odd, a, b)
    above = eye + jnp.where(odd, b, a)
    below2 = jnp.where(slab >= 2, eye + below2_ref[...], 0.0)
    put(left_b_out, split(below.T))
    put(left_a_out, split(here))
    for columns, out, block in (
        (slice(0, 2 * width), right_b_out, below),
        (slice(2 * width, 4 * width), right_b_out, below2.T),
        (slice(0, 2 * width), right_a_out, here.T),
        (slice(2 * width, 4 * width), right_a_out, above),
    ):
        put(out, split(stack_rows(real_tiles(block, wide_ref))), columns)
    count = slab_ref[1]
    for i in range(energies):
        for j in range(i, energies):
            total = jnp.int32(0)
            for p in range(pairs_ref.shape[0]):
                e1, e2 = pairs_ref[p, 0] ^ count, pairs_ref[p, 1] ^ count
                hit = ((e1 == i) & (e2 == j)) | ((e1 == j) & (e2 == i))
                total = total + hit.astype(jnp.int32)
            weight_out[energies * i + j] = jnp.full((8, 128), total.astype(F32))


def pair(ref):
    return ref[0], ref[1]


def second_kernel(
    slab_ref, a_ref, swap_a_ref, swap_b_ref, left_b_ref, left_a_ref, right_b_ref, right_a_ref,
    a_out, l_out, u_out, p_out, x_ref,
):
    n = a_ref.shape[1]
    odd = (slab_ref[0] & 1) == 1
    swap_a, swap_b = swap_a_ref[...], swap_b_ref[...]
    below = dot3(pair(left_b_ref), split(jnp.where(odd, swap_a, swap_b)))
    both = dot3(split(below), pair(right_b_ref))
    above = dot3(pair(left_a_ref), split(jnp.where(odd, swap_b, swap_a)))
    other = dot3(split(above), pair(right_a_ref))
    a = a_ref[...] - both[:, :n] - other[:, :n]
    lower = -both[:, n:]
    upper = -other[:, n:]
    a_out[...] = a
    l_out[...] = lower
    u_out[...] = upper
    x_ref[...] = a
    invert_in_place(x_ref)
    x = split(x_ref[...])
    p_out[0] = dot3(x, split(stack_rows(upper)))
    p_out[1] = dot3(x, split(stack_rows(lower)))


def sides(slab_ref, distance, swap_a_ref, swap_b_ref, i, j):
    low = (slab_ref[0] & distance) == 0
    below = jnp.where(low, swap_b_ref[i], swap_a_ref[i])
    above = jnp.where(low, swap_a_ref[j], swap_b_ref[j])
    return below, above


def middle_kernel(distance, slab_ref, a_ref, l_ref, u_ref, swap_a_ref, swap_b_ref, a_out, l_out, u_out, p_out, x_ref):
    lower, upper = split(l_ref[...]), split(u_ref[...])
    forward, backward = sides(slab_ref, distance, swap_a_ref, swap_b_ref, 0, 1)
    a = a_ref[...] - dot3(lower, split(stack_rows(forward)))
    a = a - dot3(upper, split(stack_rows(backward)))
    backward, forward = sides(slab_ref, distance, swap_a_ref, swap_b_ref, 1, 0)
    new_lower = -dot3(lower, split(stack_rows(backward)))
    new_upper = -dot3(upper, split(stack_rows(forward)))
    a_out[...] = a
    l_out[...] = new_lower
    u_out[...] = new_upper
    x_ref[...] = a
    invert_in_place(x_ref)
    x = split(x_ref[...])
    p_out[0] = dot3(x, split(stack_rows(new_upper)))
    p_out[1] = dot3(x, split(stack_rows(new_lower)))


def pair_kernel(distance, half, slab_ref, a_ref, l_ref, u_ref, swap_a_ref, swap_b_ref, a_out, c_out, w_out, x_ref):
    first = slab_ref[0] < half
    forward, backward = sides(slab_ref, distance, swap_a_ref, swap_b_ref, 0, 1)
    a = a_ref[...] - product(l_ref[...], forward) - product(u_ref[...], backward)
    backward, forward = sides(slab_ref, distance, swap_a_ref, swap_b_ref, 1, 0)
    left = jnp.where(first, u_ref[...], l_ref[...])
    link = -product(left, jnp.where(first, forward, backward))
    a_out[...] = a
    c_out[...] = link
    x_ref[...] = a
    invert_in_place(x_ref)
    w_out[...] = product(x_ref[...], link)


def last_kernel(a_ref, c_ref, w_ref, g_out, x_ref):
    x_ref[...] = a_ref[...] - product(c_ref[...], w_ref[...])
    invert_in_place(x_ref)
    g_out[...] = from_tiles(x_ref[...])


def sigma_kernel(pair_count, weight_ref, scale_ref, *refs):
    green, out_ref, wide_ref = refs[:-2], refs[-2], refs[-1]
    count = len(green)
    width = scale_ref.shape[0]
    wide_ref[:, :width] = scale_ref[...] * (1.0 / pair_count)
    rows = HALF
    low = iota((rows, 128), 1) < HALF

    def weight(i, j):
        return jnp.broadcast_to(weight_ref[count * i + j, :1, :], (rows, 128))

    def combine(z):
        total = None
        for i in range(count):
            inner = None
            for j in range(i, count):
                w = weight(i, j)
                term = (w * z[j][0], w * z[j][1])
                inner = term if inner is None else cadd(inner, term)
            term = cmul(z[i], inner)
            total = term if total is None else cadd(total, term)
        return total

    for r in range(0, width, rows):
        here = slice(r, r + rows)
        main, rest = [], []
        for g in green:
            t0, t1, t2 = g[here, :128], g[here, 128:256], g[here, 256:]
            main.append((t0, pltpu.roll(jnp.where(low, t2, t1), HALF, 1)))
            rest.append((t1, pltpu.roll(t2, HALF, 1)))
        s0, s1 = wide_ref[here, :128], wide_ref[here, 128:]
        m = combine(main)
        q = combine(rest)
        mi = pltpu.roll(m[1] * s0, HALF, 1)
        qi = pltpu.roll(q[1] * s1, HALF, 1)
        out_ref[here, :128] = m[0] * s0
        out_ref[here, 128:256] = jnp.where(low, q[0] * s1, mi)
        out_ref[here, 256:] = jnp.where(low, mi, qi)


def call(kernel, ins, outs, scratch=(), scalars=0, held=0):
    ins = [keep(x) if scalars <= i < scalars + held else x for i, x in enumerate(ins)]
    vmem = pl.BlockSpec(memory_space=pltpu.VMEM)
    smem = pl.BlockSpec(memory_space=pltpu.SMEM)
    outs = tuple(pltpu.VMEM(o, F32) if isinstance(o, tuple) else o for o in outs)
    return pl.pallas_call(
        kernel,
        out_shape=outs,
        in_specs=[smem] * scalars + [vmem] * (len(ins) - scalars),
        out_specs=tuple(vmem for _ in outs),
        scratch_shapes=[pltpu.VMEM(s, F32) for s in scratch],
        compiler_params=pltpu.CompilerParams(vmem_limit_bytes=56 * 2**20),
    )(*ins)


def keep(x):
    return pltpu.with_memory_space_constraint(x, pltpu.VMEM)


def swaps(value, distance):
    count = lax.axis_size("slab")
    near = [(s, s ^ distance) for s in range(count)]
    far = [(s, s + distance if s & distance else s - distance) for s in range(count)]
    far = [(s, t) for s, t in far if 0 <= t < count]
    near = lax.ppermute(value, "slab", near)
    far = lax.ppermute(value, "slab", far)
    return keep(near), keep(far)


def program(energy_sq, broadening, onsite, coupling, sigma_in, anharmonic, energy_pairs):
    width = onsite.shape[-1]
    block = (width, 2 * width)
    count = lax.axis_size("slab")
    energies = lax.axis_size("energy")
    level_count = count.bit_length() - 1
    slab = lax.axis_index("slab").astype(jnp.int32)
    place = jnp.stack([slab, lax.axis_index("energy").astype(jnp.int32)])
    here = coupling[0]
    bond_a, bond_b = swaps(here, 1)
    a, x0 = call(
        first_kernel, (energy_sq, broadening, onsite[0], sigma_in[0, 0]), (block, block),
        scratch=((width, 256),), scalars=2,
    )
    swap_a, swap_b = swaps(x0, 1)
    below2 = keep(lax.ppermute(here, "slab", [(s, s + 2) for s in range(count - 2)]))
    wide = pltpu.VMEM((2, 2 * width, 4 * width), BF16)
    real = pltpu.VMEM((2, width, width), BF16)
    *operands, weight = call(
        functools.partial(prepare_kernel, energies),
        (place, energy_pairs[0], here, bond_a, bond_b, below2),
        (real, real, wide, wide, (energies**2, 8, 128)), scratch=((width, 256),), scalars=2,
    )
    a, lower, upper, payload = call(
        second_kernel, (place, a, swap_a, swap_b, *operands),
        (block, block, block, (2,) + block), scratch=(block,), scalars=1, held=7,
    )
    for level in range(1, level_count - 1):
        distance = 2**level
        swap_a, swap_b = swaps(payload, distance)
        if level < level_count - 2:
            a, lower, upper, payload = call(
                functools.partial(middle_kernel, distance), (place, a, lower, upper, swap_a, swap_b),
                (block, block, block, (2,) + block), scratch=(block,), scalars=1, held=5,
            )
    half = count // 2
    a, link, w = call(
        functools.partial(pair_kernel, half // 2, half), (place, a, lower, upper, swap_a, swap_b),
        (block, block, block), scratch=(block,), scalars=1, held=5,
    )
    w = keep(lax.ppermute(w, "slab", [(s, s ^ half) for s in range(count)]))
    result = jax.ShapeDtypeStruct(block, F32)
    (green,) = call(last_kernel, (a, link, w), (result,), scratch=(block,), held=3)

    table = {0: green}
    step = energies // 2
    while step:
        for offset in list(table):
            table[offset ^ step] = keep(
                lax.ppermute(table[offset], "energy", [(e, e ^ step) for e in range(energies)])
            )
        step //= 2
    (sigma,) = call(
        functools.partial(sigma_kernel, energy_pairs.shape[1]),
        (weight, anharmonic[0], *(table[o] for o in range(energies))), (result,),
        scratch=((width, 256),), held=1,
    )
    return green[None, None], sigma[None, None]


def solution(mesh):
    in_specs = (
        P("energy"),
        P("energy"),
        P("slab", None, None),
        P("slab", None, None),
        P("energy", "slab", None, None),
        P("slab", None, None),
        P("energy", None, None),
    )
    out_specs = (P("energy", "slab", None, None), P("energy", "slab", None, None))
    return jax.shard_map(program, mesh=mesh, in_specs=in_specs, out_specs=out_specs, check_vma=False)
```
